32 devices in a mesh: dom: 16 (over z, y, core), vol: 2 (over x).
Axes of the slice: x: 2, y: 2, z: 4, core: 2. Of those that a mesh axis runs over, the one named last changes fastest.
Arguments:
- images: bfloat16 [8192, 2, 2048], P('dom', None, 'vol'), may hold values from -8 to 8
- ctf_gain: bfloat16 [8192, 2048], P('dom', 'vol'), may hold values from -1 to 1
- orientation: int32 [8192, 8], P('dom'), may hold values from 0 to 15
- class_ids: int32 [8192, 8], P('dom'), may hold values from 0 to 15
- slice_index: int32 [16, 2048], P(None, 'vol'), may hold values from 0 to 131071, as said below
- volume: bfloat16 [16, 2, 2, 65536], P(None, None, 'vol', 'dom'), may hold values from -5 to 5
- noise_power: float32 [2048], P('vol'), may hold values from 40 to 160
- log_prior: float32 [16], replicated, may hold values from -1.5 to 1.5
- prior_precision: float32 [2, 65536], P('vol', 'dom'), may hold values from 0.5 to 4
Outputs:
- new_volume: bfloat16 [16, 2, 2, 65536], P(None, None, 'vol', 'dom')
- noise_update: float32 [2048], P('vol')
- occupancy: float32 [16], replicated
The draws below stay inside these ranges and needn't reach their ends.
Inputs may be any that keep to these rules, and one draw needn't show every extreme that they name: `slice_index`: the coefficients of band b, columns b * 1024 to (b + 1) * 1024 - 1, map to voxels b * 65536 to (b + 1) * 65536 - 1.
All inputs are finite; a program needn't handle non-finite values.
Results may differ from the reference program's by a relative error of at most 0.012.
Values may be sent and summed in bfloat16 or wider, within the bound.
A program may use at most 128 MiB of HBM per device.

```python
import math
import jax
import jax.numpy as jnp
from jax import lax

CLASSES = 16
NPIX = 2048
VOX = 131072
ORIENTS = 16
HYPOTHESES = 8
PART_DEV = 512
PARTICLES = 8192
SHELLS = 2
SHELL_VOX = 65536
SHELL_PIX = 1024
N_DOM = 16


def base_volume(key):
    fresh_key = jax.random.fold_in(key, 101)
    volume_shape = (CLASSES, 2, SHELLS, SHELL_VOX)
    values = jnp.clip(jax.random.normal(fresh_key, volume_shape), -5.0, 5.0)
    return values.astype(jnp.float32).astype(jnp.bfloat16)


def base_slice_index(key):
    fresh_key = jax.random.fold_in(key, 102)
    offsets = jax.random.randint(fresh_key, (ORIENTS, SHELLS, SHELL_PIX), 0, SHELL_VOX)
    base_voxel = jnp.arange(SHELLS, dtype=jnp.int32)[None, :, None] * SHELL_VOX
    flat_index = (offsets + base_voxel).reshape(ORIENTS, NPIX).astype(jnp.int32)
    flat_index = flat_index.at[0, 0].set(0)
    flat_index = flat_index.at[ORIENTS - 1, NPIX - 1].set(VOX - 1)
    return flat_index


def base_ctf(key):
    fresh_key = jax.random.fold_in(key, 103)
    values = jax.random.uniform(fresh_key, (PARTICLES, NPIX), minval=-1.0, maxval=1.0)
    return values.astype(jnp.float32).astype(jnp.bfloat16)


def base_orientation(key):
    fresh_key = jax.random.fold_in(key, 104)
    chosen_orients = jax.random.randint(fresh_key, (PARTICLES, HYPOTHESES), 0, ORIENTS).astype(jnp.int32)
    chosen_orients = chosen_orients.at[0, 0].set(0)
    return chosen_orients.at[0, 1].set(ORIENTS - 1)


def base_classes(key):
    rank_key = jax.random.fold_in(key, 105)
    order_key = jax.random.fold_in(key, 106)
    weight_list = [720720 // (position + 1) for position in range(CLASSES)]
    total_weight = sum(weight_list)
    weights = jnp.array(weight_list, dtype=jnp.int32)
    bounds = jnp.cumsum(weights).astype(jnp.int32)
    uniform_ints = jax.random.randint(rank_key, (PARTICLES, HYPOTHESES), 0, total_weight).astype(jnp.int32)
    ranks = jnp.sum((uniform_ints[:, :, None] >= bounds[None, None, :]).astype(jnp.int32), axis=2).astype(jnp.int32)
    ordering = jax.random.permutation(order_key, CLASSES).astype(jnp.int32)
    classes_out = jnp.take(ordering, ranks).astype(jnp.int32)
    classes_out = classes_out.at[0, 0].set(0)
    return classes_out.at[0, 1].set(CLASSES - 1)


def draw_volume(key, part):
    return base_volume(key)


def draw_slice_index(key, part):
    return base_slice_index(key)


def draw_ctf_gain(key, part):
    return base_ctf(key)


def draw_orientation(key, part):
    return base_orientation(key)


def draw_class_ids(key, part):
    return base_classes(key)


def draw_images(key, part):
    volume_flat = base_volume(key).astype(jnp.float32).reshape(CLASSES, 2, VOX)
    sections = jnp.take(volume_flat, base_slice_index(key), axis=2)
    section_table = jnp.transpose(sections, (0, 2, 1, 3)).reshape(CLASSES * ORIENTS, 2, NPIX)
    hypotheses_all = (base_classes(key) * ORIENTS + base_orientation(key)).astype(jnp.int32)
    chosen_slot = jax.random.randint(jax.random.fold_in(key, 107), (PARTICLES, 1), 0, HYPOTHESES).astype(jnp.int32)
    true_hypothesis = jnp.take_along_axis(hypotheses_all, chosen_slot, axis=1)[:, 0]
    signal = section_table[true_hypothesis]
    gain_values = base_ctf(key).astype(jnp.float32)
    noise_key = jax.random.fold_in(key, 108)
    noise_part = jnp.clip(jax.random.normal(noise_key, (PARTICLES, 2, NPIX)), -6.0, 6.0)
    images_value = noise_part + 0.15 * gain_values[:, None, :] * signal
    return images_value.astype(jnp.float32).astype(jnp.bfloat16)


def block_levels(stream_key, shape, cuts, smallest, top_value):
    def one(axis_at, shards_of):
        heights = jax.random.uniform(jax.random.fold_in(jax.random.fold_in(stream_key, 6), axis_at), (shards_of,), jnp.float32, smallest / len(cuts), top_value / len(cuts))
        return jnp.repeat(jnp.exp(heights), shape[axis_at] // shards_of).reshape((-1,) + (1,) * (len(shape) - axis_at - 1))

    level = one(*cuts[0])
    for cut in cuts[1:]:
        level = level * one(*cut)
    return level


def setup_inputs(seed: int = 0) -> dict:
    arg_keys = jax.random.split(jax.random.key(seed), 10)
    images = draw_images(jax.random.fold_in(arg_keys[9], 71), 0)
    ctf_gain = draw_ctf_gain(jax.random.fold_in(arg_keys[9], 71), 0)
    orientation = draw_orientation(jax.random.fold_in(arg_keys[9], 71), 0)
    class_ids = draw_class_ids(jax.random.fold_in(arg_keys[9], 71), 0)
    slice_index = draw_slice_index(jax.random.fold_in(arg_keys[9], 71), 0)
    volume = draw_volume(jax.random.fold_in(arg_keys[9], 71), 0)
    noise_power = jnp.clip(jnp.exp(math.log(160.0) - 1.3862944 * jax.random.uniform(arg_keys[6], (NPIX,), jnp.float32) ** block_levels(arg_keys[6], (NPIX,), ((0, 2),), -0.2, 0.2)), 40.0, 160.0)
    log_prior = jnp.clip(jax.random.uniform(arg_keys[7], (CLASSES,), jnp.float32, -1.5, 1.5), -1.5, 1.5)
    prior_precision = jnp.clip(jnp.exp(math.log(4.0) - 2.0794415 * jax.random.uniform(arg_keys[8], (SHELLS, SHELL_VOX), jnp.float32) ** block_levels(arg_keys[8], (SHELLS, SHELL_VOX), ((0, 2), (1, 16)), -0.2, 0.2)), 0.5, 4.0)
    return dict(images=images, ctf_gain=ctf_gain, orientation=orientation, class_ids=class_ids, slice_index=slice_index, volume=volume, noise_power=noise_power, log_prior=log_prior, prior_precision=prior_precision)


def reference(images, ctf_gain, orientation, class_ids, slice_index, volume, noise_power, log_prior, prior_precision):
    hypo_count = CLASSES * ORIENTS
    flat_volume = volume.reshape(CLASSES, 2, VOX)
    slices = jnp.take(flat_volume, slice_index, axis=2)
    projected = jnp.transpose(slices, (0, 2, 1, 3)).reshape(hypo_count, 2 * NPIX)
    power_table = jnp.sum(jnp.square(slices.astype(jnp.float32)), axis=1).reshape(hypo_count, NPIX).astype(jnp.bfloat16)
    earlier = jnp.tril(jnp.ones((HYPOTHESES, HYPOTHESES), dtype=bool), -1)
    row_ids = jnp.broadcast_to(jnp.arange(PART_DEV, dtype=jnp.int32)[:, None], (PART_DEV, HYPOTHESES))

    def step_block(totals, block_in):
        data_acc, weight_acc, noise_acc, occ_acc = totals
        image_blk, gain_blk, orient_blk, class_blk = block_in
        image_f32 = image_blk.astype(jnp.float32)
        gain_f32 = gain_blk.astype(jnp.float32)
        weighted = (gain_f32[:, None, :] * image_f32 / noise_power).astype(jnp.bfloat16).reshape(PART_DEV, 2 * NPIX)
        damped = (gain_f32 * gain_f32 / (2.0 * noise_power)).astype(jnp.bfloat16)
        hypothesis = (class_blk * ORIENTS + orient_blk).astype(jnp.int32)
        picked = projected[hypothesis]
        picked_power = power_table[hypothesis]
        cross_term = jnp.sum(weighted.astype(jnp.float32)[:, None, :] * picked.astype(jnp.float32), axis=2)
        energy = jnp.sum(damped.astype(jnp.float32)[:, None, :] * picked_power.astype(jnp.float32), axis=2)
        scores = log_prior[class_blk] + (cross_term - energy)
        posterior = jax.nn.softmax(scores, axis=1)
        member = jnp.zeros((PART_DEV, hypo_count), jnp.float32).at[row_ids, hypothesis].add(posterior)
        member_bf16 = member.astype(jnp.bfloat16)
        repeated = jnp.any((hypothesis[:, :, None] == hypothesis[:, None, :]) & earlier[None], axis=2)
        share = jnp.where(repeated, 0.0, jnp.take_along_axis(member_bf16, hypothesis, axis=1).astype(jnp.float32))
        carried = (gain_f32[:, None, :] * image_f32).astype(jnp.bfloat16).reshape(PART_DEV, 2 * NPIX)
        gain_square = (gain_f32 * gain_f32).astype(jnp.bfloat16)
        flat_hypo = hypothesis.reshape(-1)
        data_terms = (share[:, :, None] * carried.astype(jnp.float32)[:, None, :]).reshape(PART_DEV * HYPOTHESES, 2 * NPIX)
        weight_terms = (share[:, :, None] * gain_square.astype(jnp.float32)[:, None, :]).reshape(PART_DEV * HYPOTHESES, NPIX)
        data_acc = data_acc + jax.ops.segment_sum(data_terms, flat_hypo, num_segments=hypo_count)
        weight_acc = weight_acc + jax.ops.segment_sum(weight_terms, flat_hypo, num_segments=hypo_count)
        mean_proj = jnp.sum(share[:, :, None] * picked.astype(jnp.float32), axis=1).reshape(PART_DEV, 2, NPIX)
        mean_power = jnp.sum(share[:, :, None] * picked_power.astype(jnp.float32), axis=1)
        residual = jnp.sum(image_f32 * image_f32, axis=1) - 2.0 * gain_f32 * jnp.sum(image_f32 * mean_proj, axis=1) + gain_f32 * gain_f32 * mean_power
        noise_acc = noise_acc + jnp.sum(residual, axis=0)
        occ_acc = occ_acc + jnp.sum(member.reshape(PART_DEV, CLASSES, ORIENTS), axis=(0, 2))
        return (data_acc, weight_acc, noise_acc, occ_acc), None

    block_in = (images.reshape(N_DOM, PART_DEV, 2, NPIX), ctf_gain.reshape(N_DOM, PART_DEV, NPIX),
                orientation.reshape(N_DOM, PART_DEV, HYPOTHESES), class_ids.reshape(N_DOM, PART_DEV, HYPOTHESES))
    start = (jnp.zeros((hypo_count, 2 * NPIX), jnp.float32), jnp.zeros((hypo_count, NPIX), jnp.float32),
             jnp.zeros((NPIX,), jnp.float32), jnp.zeros((CLASSES,), jnp.float32))
    totals, _ = lax.scan(step_block, start, block_in)
    data_acc, weight_acc, noise_acc, occ_acc = totals
    noise_update = noise_acc / (2.0 * PARTICLES)
    occupancy = occ_acc / PARTICLES
    data_grid = jnp.transpose(data_acc.reshape(CLASSES, ORIENTS, 2, NPIX), (0, 2, 1, 3))
    data_sum = jnp.zeros((CLASSES, 2, VOX), jnp.float32).at[:, :, slice_index].add(data_grid)
    weight_sum = jnp.zeros((CLASSES, VOX), jnp.float32).at[:, slice_index].add(weight_acc.reshape(CLASSES, ORIENTS, NPIX))
    denominator = weight_sum + prior_precision.reshape(VOX)
    new_volume = (data_sum / denominator[:, None, :]).astype(jnp.bfloat16).reshape(CLASSES, 2, SHELLS, SHELL_VOX)
    return new_volume, noise_update, occupancy
```

```python
import functools

import jax
import jax.numpy as jnp
from jax import lax
from jax.experimental import pallas as pl
from jax.experimental.pallas import tpu as pltpu
from jax.sharding import PartitionSpec as P

LANES = 256
BIG = 48 << 20
NT = (((1,), (1,)), ((), ()))


def voxel_base(shell_vox, vox_dev):
    return lax.axis_index("vol") * shell_vox + lax.axis_index("dom") * vox_dev


def gather_kernel(shell_vox, vox_dev, index_ref, vol_ref, out_ref, stack_ref):
    orient = pl.program_id(0)
    groups = vox_dev // LANES
    rows = vol_ref.shape[0]

    @pl.when(orient == 0)
    def _():
        for q in range(groups):
            stack_ref[q * rows : (q + 1) * rows, :] = vol_ref[:, q * LANES : (q + 1) * LANES]

    rel = index_ref[pl.ds(orient, 1), :] - voxel_base(shell_vox, vox_dev)
    low = rel & (LANES - 1)
    high = rel >> 8
    pix = rel.shape[1]
    step = 256
    for start in range(0, pix, step):
        low_c = low[:, start : start + step]
        high_c = high[:, start : start + step]
        hot = jnp.where(
            lax.broadcasted_iota(jnp.int32, (LANES, step), 0) == low_c, 1.0, 0.0
        ).astype(jnp.bfloat16)
        found = jnp.dot(stack_ref[...], hot, preferred_element_type=jnp.float32)
        total = jnp.zeros((rows, step), jnp.float32)
        for q in range(groups):
            total = jnp.where(high_c == q, found[q * rows : (q + 1) * rows], total)
        half = rows // 2
        out_ref[0, 0, :, start : start + step] = total[:half].astype(jnp.bfloat16)
        out_ref[1, 0, :, start : start + step] = total[half:].astype(jnp.bfloat16)


def fit_kernel(proj_ref, weighted_ref, damped_ref, hypo_ref, out_ref):
    p0 = proj_ref[0]
    p1 = proj_ref[1]
    f0 = p0.astype(jnp.float32)
    f1 = p1.astype(jnp.float32)
    power = (f0 * f0 + f1 * f1).astype(jnp.bfloat16)
    value = lax.dot_general(p0, weighted_ref[0], NT, preferred_element_type=jnp.float32)
    value += lax.dot_general(p1, weighted_ref[1], NT, preferred_element_type=jnp.float32)
    value -= lax.dot_general(power, damped_ref[...], NT, preferred_element_type=jnp.float32)
    ids = lax.broadcasted_iota(jnp.int32, value.shape, 0)
    for k in range(hypo_ref.shape[0]):
        out_ref[k : k + 1, :] = jnp.sum(
            jnp.where(hypo_ref[k : k + 1, :] == ids, value, 0.0), axis=0, keepdims=True
        )


def member_kernel(
    prior_ref, fit_ref, hypo_ref, proj_ref, carried_ref, square_ref, energy_ref,
    table_ref, noise_ref, occ_ref,
):
    hypo = hypo_ref[...]
    classes = prior_ref.shape[0]
    class_of = lax.rem(hypo, classes)
    scores = fit_ref[...]
    for c in range(classes):
        scores += jnp.where(class_of == c, prior_ref[c], 0.0)
    top = jnp.max(scores, axis=0, keepdims=True)
    expo = jnp.exp(scores - top)
    posterior = expo / jnp.sum(expo, axis=0, keepdims=True)
    count = proj_ref.shape[1]
    ids = lax.broadcasted_iota(jnp.int32, (count, hypo.shape[1]), 0)
    member = jnp.zeros(ids.shape, jnp.float32)
    for k in range(hypo.shape[0]):
        member += jnp.where(hypo[k : k + 1, :] == ids, posterior[k : k + 1, :], 0.0)
    occ = jnp.sum(member, axis=1, keepdims=True)
    occ_ref[...] = jnp.sum(occ.reshape(count // classes, classes, 1), axis=0)
    member16 = member.astype(jnp.bfloat16)
    pix = square_ref.shape[1]
    step = 256
    for start in range(0, pix, step):
        cols = slice(start, start + step)
        p0 = proj_ref[0, :, cols].astype(jnp.float32)
        p1 = proj_ref[1, :, cols].astype(jnp.float32)
        power = (p0 * p0 + p1 * p1).astype(jnp.bfloat16).astype(jnp.float32)
        d0 = jnp.dot(member16, carried_ref[0, :, cols], preferred_element_type=jnp.float32)
        d1 = jnp.dot(member16, carried_ref[1, :, cols], preferred_element_type=jnp.float32)
        dw = jnp.dot(member16, square_ref[:, cols], preferred_element_type=jnp.float32)
        noise_ref[:, cols] = energy_ref[:, cols] + jnp.sum(
            power * dw - 2.0 * (p0 * d0 + p1 * d1), axis=0, keepdims=True
        )
        for i, d in enumerate((d0, d1, dw)):
            table_ref[:, i * classes : (i + 1) * classes, cols] = d.astype(jnp.bfloat16).reshape(
                count // classes, classes, step
            )


def scatter_kernel(shell_vox, vox_dev, index_ref, table_ref, prior_ref, out_ref, total_ref):
    orient = pl.program_id(0)
    groups = vox_dev // LANES
    rows = table_ref.shape[1]

    @pl.when(orient == 0)
    def _():
        total_ref[...] = jnp.zeros_like(total_ref)

    rel = index_ref[pl.ds(orient, 1), :] - voxel_base(shell_vox, vox_dev)
    low = rel & (LANES - 1)
    high = rel >> 8
    pix = rel.shape[1]
    hot = jnp.where(
        lax.broadcasted_iota(jnp.int32, (LANES, pix), 0) == low, 1.0, 0.0
    ).astype(jnp.bfloat16)
    table = table_ref[0]
    parts = [
        table * jnp.where(high == q, 1.0, 0.0).astype(jnp.bfloat16) for q in range(groups)
    ]
    spread = jnp.concatenate(parts, axis=0) if groups > 1 else parts[0]
    total_ref[...] += lax.dot_general(spread, hot, NT, preferred_element_type=jnp.float32)

    @pl.when(orient == pl.num_programs(0) - 1)
    def _():
        third = rows // 3
        for q in range(groups):
            cols = slice(q * LANES, (q + 1) * LANES)
            at = q * rows
            weight = total_ref[at + 2 * third : at + rows, :] + prior_ref[:, cols]
            out_ref[0, :, cols] = (total_ref[at : at + third, :] / weight).astype(jnp.bfloat16)
            out_ref[1, :, cols] = (total_ref[at + third : at + 2 * third, :] / weight).astype(
                jnp.bfloat16
            )


def shards(
    images,
    ctf_gain,
    orientation,
    class_ids,
    slice_index,
    volume,
    noise_power,
    log_prior,
    prior_precision,
):
    groups = lax.axis_size("dom")
    part_dev = images.shape[0]
    pix = images.shape[2]
    classes = volume.shape[0]
    vox_dev = volume.shape[3]
    orients = slice_index.shape[0]
    hypos = classes * orients
    shell_vox = vox_dev * groups
    cands = orientation.shape[1]
    params = pltpu.CompilerParams(vmem_limit_bytes=BIG)
    vol_rows = jnp.transpose(volume[:, :, 0, :], (1, 0, 2)).reshape(2 * classes, vox_dev)
    found = pl.pallas_call(
        functools.partial(gather_kernel, shell_vox, vox_dev),
        grid=(orients,),
        out_shape=jax.ShapeDtypeStruct((2, orients, classes, pix), jnp.bfloat16),
        in_specs=[
            pl.BlockSpec((orients, pix), lambda o: (0, 0)),
            pl.BlockSpec((2 * classes, vox_dev), lambda o: (0, 0)),
        ],
        out_specs=pl.BlockSpec((2, 1, classes, pix), lambda o: (0, o, 0, 0)),
        scratch_shapes=[pltpu.VMEM((2 * classes * vox_dev // LANES, LANES), jnp.bfloat16)],
        compiler_params=params,
    )(slice_index, vol_rows)
    projected = lax.psum(found, "dom").reshape(2, hypos, pix)

    gain = ctf_gain.astype(jnp.float32)
    image0 = images[:, 0, :].astype(jnp.float32)
    image1 = images[:, 1, :].astype(jnp.float32)
    product0 = gain * image0
    product1 = gain * image1
    weighted = jnp.stack([product0 / noise_power, product1 / noise_power]).astype(jnp.bfloat16)
    carried = jnp.stack([product0, product1]).astype(jnp.bfloat16)
    damped = (gain * gain / (2.0 * noise_power)).astype(jnp.bfloat16)
    square = (gain * gain).astype(jnp.bfloat16)
    energy = jnp.sum(image0 * image0 + image1 * image1, axis=0, keepdims=True)
    hypo = (orientation * classes + class_ids).T

    partial_fit = pl.pallas_call(
        fit_kernel,
        out_shape=jax.ShapeDtypeStruct((cands, part_dev), jnp.float32),
        compiler_params=params,
    )(projected, weighted, damped, hypo)
    fitted = lax.psum(partial_fit, "vol")
    vmem = pl.BlockSpec(memory_space=pltpu.VMEM)
    table, noise_part, occ_part = pl.pallas_call(
        member_kernel,
        out_shape=(
            jax.ShapeDtypeStruct((orients, 3 * classes, pix), jnp.bfloat16),
            jax.ShapeDtypeStruct((1, pix), jnp.float32),
            jax.ShapeDtypeStruct((classes, 1), jnp.float32),
        ),
        in_specs=[pl.BlockSpec(memory_space=pltpu.SMEM)] + [vmem] * 6,
        compiler_params=params,
    )(log_prior, fitted, hypo, projected, carried, square, energy)
    table = lax.psum(table, "dom")
    noise_sum, occ_sum = lax.psum((noise_part[0], occ_part[:, 0]), "dom")
    particles = part_dev * groups
    noise_update = noise_sum / (2.0 * particles)
    occupancy = occ_sum / particles
    volume_out = pl.pallas_call(
        functools.partial(scatter_kernel, shell_vox, vox_dev),
        grid=(orients,),
        out_shape=jax.ShapeDtypeStruct((2, classes, vox_dev), jnp.bfloat16),
        in_specs=[
            pl.BlockSpec((orients, pix), lambda o: (0, 0)),
            pl.BlockSpec((1, 3 * classes, pix), lambda o: (o, 0, 0)),
            pl.BlockSpec((1, vox_dev), lambda o: (0, 0)),
        ],
        out_specs=pl.BlockSpec((2, classes, vox_dev), lambda o: (0, 0, 0)),
        scratch_shapes=[pltpu.VMEM((3 * classes * vox_dev // LANES, LANES), jnp.float32)],
        compiler_params=params,
    )(slice_index, table, prior_precision)
    new_volume = jnp.transpose(volume_out, (1, 0, 2))[:, :, None, :]
    return (new_volume, noise_update, occupancy)


def solution(mesh):
    in_specs = (
        P("dom", None, "vol"),
        P("dom", "vol"),
        P("dom", None),
        P("dom", None),
        P(None, "vol"),
        P(None, None, "vol", "dom"),
        P("vol"),
        P(),
        P("vol", "dom"),
    )
    out_specs = (P(None, None, "vol", "dom"), P("vol"), P())
    return jax.shard_map(shards, mesh=mesh, in_specs=in_specs, out_specs=out_specs, check_vma=False)
```

```python
import functools

import jax
import jax.numpy as jnp
from jax import lax
from jax.experimental import pallas as pl
from jax.experimental.pallas import tpu as pltpu
from jax.sharding import PartitionSpec as P

LANES = 256
BIG = 48 << 20
NT = (((1,), (1,)), ((), ()))


def voxel_base(shell_vox, vox_dev):
    return lax.axis_index("vol") * shell_vox + lax.axis_index("dom") * vox_dev


def gather_kernel(shell_vox, vox_dev, index_ref, vol_ref, out_ref, stack_ref):
    orient = pl.program_id(0)
    groups = vox_dev // LANES
    rows = vol_ref.shape[0]

    @pl.when(orient == 0)
    def _():
        for q in range(groups):
            stack_ref[q * rows : (q + 1) * rows, :] = vol_ref[:, q * LANES : (q + 1) * LANES]

    rel = index_ref[pl.ds(orient, 1), :] - voxel_base(shell_vox, vox_dev)
    low = rel & (LANES - 1)
    high = rel >> 8
    pix = rel.shape[1]
    step = 256
    for start in range(0, pix, step):
        low_c = low[:, start : start + step]
        high_c = high[:, start : start + step]
        hot = jnp.where(
            lax.broadcasted_iota(jnp.int32, (LANES, step), 0) == low_c, 1.0, 0.0
        ).astype(jnp.bfloat16)
        found = jnp.dot(stack_ref[...], hot, preferred_element_type=jnp.float32)
        total = jnp.zeros((rows, step), jnp.float32)
        for q in range(groups):
            total = jnp.where(high_c == q, found[q * rows : (q + 1) * rows], total)
        out_ref[0, :, start : start + step] = total.astype(jnp.bfloat16)


def scatter_kernel(shell_vox, vox_dev, index_ref, table_ref, prior_ref, out_ref, total_ref):
    orient = pl.program_id(0)
    groups = vox_dev // LANES
    rows = table_ref.shape[1]

    @pl.when(orient == 0)
    def _():
        total_ref[...] = jnp.zeros_like(total_ref)

    rel = index_ref[pl.ds(orient, 1), :] - voxel_base(shell_vox, vox_dev)
    low = rel & (LANES - 1)
    high = rel >> 8
    pix = rel.shape[1]
    hot = jnp.where(
        lax.broadcasted_iota(jnp.int32, (LANES, pix), 0) == low, 1.0, 0.0
    ).astype(jnp.bfloat16)
    table = table_ref[0]
    parts = [
        table * jnp.where(high == q, 1.0, 0.0).astype(jnp.bfloat16) for q in range(groups)
    ]
    spread = jnp.concatenate(parts, axis=0) if groups > 1 else parts[0]
    total_ref[...] += lax.dot_general(spread, hot, NT, preferred_element_type=jnp.float32)

    @pl.when(orient == pl.num_programs(0) - 1)
    def _():
        third = rows // 3
        for q in range(groups):
            cols = slice(q * LANES, (q + 1) * LANES)
            at = q * rows
            weight = total_ref[at + 2 * third : at + rows, :] + prior_ref[:, cols]
            out_ref[0, :, cols] = (total_ref[at : at + third, :] / weight).astype(jnp.bfloat16)
            out_ref[1, :, cols] = (total_ref[at + third : at + 2 * third, :] / weight).astype(
                jnp.bfloat16
            )


MESH = pl.DeviceIdType.MESH
PARTS = 2


def level_bit(level):
    me = lax.axis_index("dom")
    return lax.rem(me // (1 << level), 2)


def partner(level):
    return lax.axis_index("dom") + (1 - 2 * level_bit(level)) * (1 << level)


def greet(levels):
    barrier = pltpu.get_barrier_semaphore()
    for level in range(levels):
        pl.semaphore_signal(barrier, inc=1, device_id={"dom": partner(level)}, device_id_type=MESH)
    pl.semaphore_wait(barrier, levels)


def send(src, dst, send_sem, recv_sem, at, level):
    copy = pltpu.make_async_remote_copy(
        src_ref=src,
        dst_ref=dst,
        send_sem=send_sem.at[at],
        recv_sem=recv_sem.at[at],
        device_id={"dom": partner(level)},
        device_id_type=MESH,
    )
    copy.start()
    return copy


class Exchange:
    def __init__(self, levels, first_ref, full_ref, recv_ref, send_sem, recv_sem):
        self.levels = levels
        self.first, self.full, self.recv = first_ref, full_ref, recv_ref
        self.sems = (send_sem, recv_sem)
        self.width = full_ref.shape[2] // PARTS
        self.low = [0]
        self.size = [1 << levels]
        for level in range(levels):
            half = self.size[-1] // 2
            self.low.append(self.low[-1] + level_bit(level) * half)
            self.size.append(half)
        self.slot = [self.size[0] - self.size[level] for level in range(levels)]

    def cols(self, part):
        return pl.ds(part * self.width, self.width)

    def source(self, level, at):
        if level == 0:
            return self.first, at
        return self.recv, self.slot[level - 1] + at - self.low[level]

    def scatter_start(self, level, part):
        half = self.size[level + 1]
        source, away = self.source(level, self.fresh(level))
        return send(
            source.at[pl.ds(away, half), :, self.cols(part)],
            self.recv.at[pl.ds(self.slot[level], half), :, self.cols(part)],
            *self.sems,
            level * PARTS + part,
            level,
        )

    def scatter_add(self, level, part):
        half = self.size[level + 1]
        for i in range(half):
            source, at = self.source(level, self.low[level + 1] + i)
            slot = self.slot[level] + i
            total = source[at, :, self.cols(part)] + self.recv[slot, :, self.cols(part)]
            if half > 1:
                self.recv[slot, :, self.cols(part)] = total
            else:
                self.full[self.low[level + 1], :, self.cols(part)] = total

    def gather_start(self, level, part):
        held = pl.ds(self.low[level + 1], self.size[level + 1])
        view = self.full.at[held, :, self.cols(part)]
        return send(
            view, view, *self.sems, (self.levels + level) * PARTS + part, level
        )

    def fresh(self, level):
        return self.low[level] + (1 - level_bit(level)) * self.size[level + 1]


def table_kernel(
    shell_vox, vox_dev, levels, index_ref, vol_ref, full_ref,
    stack_ref, first_ref, recv_ref, send_sem, recv_sem,
):
    groups = vox_dev // LANES
    rows = vol_ref.shape[0]
    pix = index_ref.shape[1]
    step = 256
    greet(levels)
    for q in range(groups):
        stack_ref[q * rows : (q + 1) * rows, :] = vol_ref[:, q * LANES : (q + 1) * LANES]
    base = voxel_base(shell_vox, vox_dev)

    def lookup(orient):
        rel = index_ref[pl.ds(orient, 1), :] - base
        low = rel & (LANES - 1)
        high = rel >> 8
        for start in range(0, pix, step):
            low_c = low[:, start : start + step]
            high_c = high[:, start : start + step]
            hot = jnp.where(
                lax.broadcasted_iota(jnp.int32, (LANES, step), 0) == low_c, 1.0, 0.0
            ).astype(jnp.bfloat16)
            found = jnp.dot(stack_ref[...], hot, preferred_element_type=jnp.float32)
            total = jnp.zeros((rows, step), jnp.float32)
            for q in range(groups):
                total = jnp.where(high_c == q, found[q * rows : (q + 1) * rows], total)
            first_ref[orient, :, start : start + step] = total.astype(jnp.bfloat16)

    ex = Exchange(levels, first_ref, full_ref, recv_ref, send_sem, recv_sem)
    half = ex.size[1]
    away = ex.fresh(0)

    @pl.loop(0, half)
    def _(i):
        lookup(away + i)

    copies = [ex.scatter_start(0, part) for part in range(PARTS)]

    @pl.loop(0, half)
    def _(i):
        lookup(ex.low[1] + i)

    for level in range(levels):
        for part in range(PARTS):
            copies[part].wait()
            ex.scatter_add(level, part)
            if level + 1 < levels:
                copies[part] = ex.scatter_start(level + 1, part)
            else:
                copies[part] = ex.gather_start(level, part)
    for level in range(levels - 1, -1, -1):
        for part in range(PARTS):
            copies[part].wait()
            if level > 0:
                copies[part] = ex.gather_start(level - 1, part)


def volume_kernel(
    shell_vox, vox_dev, levels, index_ref, first_ref, small_ref, prior_ref,
    out_ref, small_out_ref,
    total_ref, full_ref, recv_ref, held_ref, got_ref, send_sem, recv_sem, small_send, small_recv,
):
    groups = vox_dev // LANES
    rows = first_ref.shape[1]
    pix = index_ref.shape[1]
    greet(levels)
    base = voxel_base(shell_vox, vox_dev)
    ex = Exchange(levels, first_ref, full_ref, recv_ref, send_sem, recv_sem)
    copies = [ex.scatter_start(0, part) for part in range(PARTS)]
    held_ref[0] = small_ref[...]
    small = send(held_ref.at[0], got_ref.at[0], small_send, small_recv, 0, 0)
    total_ref[...] = jnp.zeros_like(total_ref)

    def spread(orient):
        rel = index_ref[pl.ds(orient, 1), :] - base
        low = rel & (LANES - 1)
        high = rel >> 8
        hot = jnp.where(
            lax.broadcasted_iota(jnp.int32, (LANES, pix), 0) == low, 1.0, 0.0
        ).astype(jnp.bfloat16)
        table = full_ref[orient]
        parts = [
            table * jnp.where(high == q, 1.0, 0.0).astype(jnp.bfloat16) for q in range(groups)
        ]
        wide = jnp.concatenate(parts, axis=0) if groups > 1 else parts[0]
        total_ref[...] += lax.dot_general(wide, hot, NT, preferred_element_type=jnp.float32)

    for level in range(levels):
        for part in range(PARTS):
            copies[part].wait()
            ex.scatter_add(level, part)
            if level + 1 < levels:
                copies[part] = ex.scatter_start(level + 1, part)
            else:
                copies[part] = ex.gather_start(level, part)
        small.wait()
        held_ref[level + 1] = held_ref[level] + got_ref[level]
        if level + 1 < levels:
            small = send(
                held_ref.at[level + 1], got_ref.at[level + 1], small_send, small_recv,
                level + 1, level + 1,
            )
    small_out_ref[...] = held_ref[levels]
    spread(ex.low[levels])
    for level in range(levels - 1, -1, -1):
        for part in range(PARTS):
            copies[part].wait()
            if level > 0:
                copies[part] = ex.gather_start(level - 1, part)

        @pl.loop(0, ex.size[level + 1])
        def _(i, level=level):
            spread(ex.fresh(level) + i)

    third = rows // 3
    for q in range(groups):
        cols = slice(q * LANES, (q + 1) * LANES)
        at = q * rows
        weight = total_ref[at + 2 * third : at + rows, :] + prior_ref[:, cols]
        out_ref[0, :, cols] = (total_ref[at : at + third, :] / weight).astype(jnp.bfloat16)
        out_ref[1, :, cols] = (total_ref[at + third : at + 2 * third, :] / weight).astype(
            jnp.bfloat16
        )


def particle_kernel(
    peers, prior_ref, hypo_ref, table_ref, weighted_ref, damped_ref, carried_ref, square_ref,
    energy_ref, out_ref, small_ref, fits_ref, send_sem, recv_sem,
):
    me = lax.axis_index("vol")
    barrier = pltpu.get_barrier_semaphore()
    for hop in range(1, peers):
        other = lax.rem(me + hop, peers)
        pl.semaphore_signal(barrier, inc=1, device_id={"vol": other}, device_id_type=MESH)
    orients, double, pix = table_ref.shape
    classes = double // 2
    count = orients * classes
    step = 256
    hypo = hypo_ref[...]
    value = jnp.zeros((count, hypo.shape[1]), jnp.float32)

    def views(cols):
        p0 = table_ref[:, :classes, cols].reshape(count, step)
        p1 = table_ref[:, classes:, cols].reshape(count, step)
        f0 = p0.astype(jnp.float32)
        f1 = p1.astype(jnp.float32)
        return p0, p1, f0, f1, (f0 * f0 + f1 * f1).astype(jnp.bfloat16)

    for start in range(0, pix, step):
        cols = slice(start, start + step)
        p0, p1, _, _, power = views(cols)
        value += lax.dot_general(p0, weighted_ref[0, :, cols], NT, preferred_element_type=jnp.float32)
        value += lax.dot_general(p1, weighted_ref[1, :, cols], NT, preferred_element_type=jnp.float32)
        value -= lax.dot_general(power, damped_ref[:, cols], NT, preferred_element_type=jnp.float32)
    ids = lax.broadcasted_iota(jnp.int32, value.shape, 0)
    rows = [
        jnp.sum(jnp.where(hypo[k : k + 1, :] == ids, value, 0.0), axis=0, keepdims=True)
        for k in range(hypo.shape[0])
    ]
    fits_ref[me] = jnp.concatenate(rows, axis=0)
    pl.semaphore_wait(barrier, peers - 1)
    copies = []
    for hop in range(1, peers):
        copy = pltpu.make_async_remote_copy(
            src_ref=fits_ref.at[me],
            dst_ref=fits_ref.at[me],
            send_sem=send_sem.at[hop - 1],
            recv_sem=recv_sem.at[hop - 1],
            device_id={"vol": lax.rem(me + hop, peers)},
            device_id_type=MESH,
        )
        copy.start()
        copies.append(copy)
    class_of = lax.rem(hypo, classes)
    scores = jnp.zeros(hypo.shape, jnp.float32)
    for c in range(classes):
        scores += jnp.where(class_of == c, prior_ref[c], 0.0)
    for copy in copies:
        copy.wait()
    fit = fits_ref[0]
    for peer in range(1, peers):
        fit += fits_ref[peer]
    scores += fit
    top = jnp.max(scores, axis=0, keepdims=True)
    expo = jnp.exp(scores - top)
    posterior = expo / jnp.sum(expo, axis=0, keepdims=True)
    member = jnp.zeros(ids.shape, jnp.float32)
    for k in range(hypo.shape[0]):
        member += jnp.where(hypo[k : k + 1, :] == ids, posterior[k : k + 1, :], 0.0)
    occ = jnp.sum(member, axis=1, keepdims=True)
    occ = jnp.sum(occ.reshape(orients, classes, 1), axis=0)
    noise_rows = pix // 128
    small_ref[noise_rows:, :] = jnp.broadcast_to(occ, (classes, 128))
    member16 = member.astype(jnp.bfloat16)
    for start in range(0, pix, step):
        cols = slice(start, start + step)
        _, _, f0, f1, power = views(cols)
        d0 = jnp.dot(member16, carried_ref[0, :, cols], preferred_element_type=jnp.float32)
        d1 = jnp.dot(member16, carried_ref[1, :, cols], preferred_element_type=jnp.float32)
        dw = jnp.dot(member16, square_ref[:, cols], preferred_element_type=jnp.float32)
        noise = energy_ref[:, cols] + jnp.sum(
            power.astype(jnp.float32) * dw - 2.0 * (f0 * d0 + f1 * d1), axis=0, keepdims=True
        )
        for i in range(step // 128):
            row = start // 128 + i
            small_ref[row : row + 1, :] = noise[:, i * 128 : (i + 1) * 128]
        for i, d in enumerate((d0, d1, dw)):
            out_ref[:, i * classes : (i + 1) * classes, cols] = d.astype(jnp.bfloat16).reshape(
                orients, classes, step
            )


def shards(
    images,
    ctf_gain,
    orientation,
    class_ids,
    slice_index,
    volume,
    noise_power,
    log_prior,
    prior_precision,
):
    groups = lax.axis_size("dom")
    peers = lax.axis_size("vol")
    part_dev = images.shape[0]
    pix = images.shape[2]
    classes = volume.shape[0]
    vox_dev = volume.shape[3]
    orients = slice_index.shape[0]
    shell_vox = vox_dev * groups
    cands = orientation.shape[1]
    levels = groups.bit_length() - 1
    direct = groups == orients and groups == 1 << levels
    params = pltpu.CompilerParams(vmem_limit_bytes=BIG)
    vmem = pl.BlockSpec(memory_space=pltpu.VMEM)
    vol_rows = jnp.transpose(volume[:, :, 0, :], (1, 0, 2)).reshape(2 * classes, vox_dev)
    stack = pltpu.VMEM((2 * classes * vox_dev // LANES, LANES), jnp.bfloat16)
    if direct:
        table = pl.pallas_call(
            functools.partial(table_kernel, shell_vox, vox_dev, levels),
            out_shape=jax.ShapeDtypeStruct((orients, 2 * classes, pix), jnp.bfloat16),
            in_specs=[vmem] * 2,
            out_specs=vmem,
            scratch_shapes=[
                stack,
                pltpu.VMEM((orients, 2 * classes, pix), jnp.bfloat16),
                pltpu.VMEM((orients - 1, 2 * classes, pix), jnp.bfloat16),
                pltpu.SemaphoreType.DMA((2 * levels * PARTS,)),
                pltpu.SemaphoreType.DMA((2 * levels * PARTS,)),
            ],
            compiler_params=pltpu.CompilerParams(
                vmem_limit_bytes=BIG, collective_id=0, has_side_effects=True
            ),
        )(slice_index, vol_rows)
    else:
        found = pl.pallas_call(
            functools.partial(gather_kernel, shell_vox, vox_dev),
            grid=(orients,),
            out_shape=jax.ShapeDtypeStruct((orients, 2 * classes, pix), jnp.bfloat16),
            in_specs=[
                pl.BlockSpec((orients, pix), lambda o: (0, 0)),
                pl.BlockSpec((2 * classes, vox_dev), lambda o: (0, 0)),
            ],
            out_specs=pl.BlockSpec((1, 2 * classes, pix), lambda o: (o, 0, 0)),
            scratch_shapes=[stack],
            compiler_params=params,
        )(slice_index, vol_rows)
        table = lax.psum(found, "dom")

    gain = ctf_gain.astype(jnp.float32)
    image0 = images[:, 0, :].astype(jnp.float32)
    image1 = images[:, 1, :].astype(jnp.float32)
    product0 = gain * image0
    product1 = gain * image1
    weighted = jnp.stack([product0 / noise_power, product1 / noise_power]).astype(jnp.bfloat16)
    carried = jnp.stack([product0, product1]).astype(jnp.bfloat16)
    damped = (gain * gain / (2.0 * noise_power)).astype(jnp.bfloat16)
    square = (gain * gain).astype(jnp.bfloat16)
    energy = jnp.sum(image0 * image0 + image1 * image1, axis=0, keepdims=True)
    hypo = (orientation * classes + class_ids).T

    noise_rows = pix // 128
    sums, small = pl.pallas_call(
        functools.partial(particle_kernel, peers),
        out_shape=(
            jax.ShapeDtypeStruct((orients, 3 * classes, pix), jnp.bfloat16),
            jax.ShapeDtypeStruct((noise_rows + classes, 128), jnp.float32),
        ),
        in_specs=[pl.BlockSpec(memory_space=pltpu.SMEM)] + [vmem] * 7,
        out_specs=(vmem, vmem),
        scratch_shapes=[
            pltpu.VMEM((peers, cands, part_dev), jnp.float32),
            pltpu.SemaphoreType.DMA((peers - 1,)),
            pltpu.SemaphoreType.DMA((peers - 1,)),
        ],
        compiler_params=pltpu.CompilerParams(
            vmem_limit_bytes=BIG, collective_id=1, has_side_effects=True
        ),
    )(log_prior, hypo, table, weighted, damped, carried, square, energy)
    out_shape = jax.ShapeDtypeStruct((2, classes, vox_dev), jnp.bfloat16)
    total = pltpu.VMEM((3 * classes * vox_dev // LANES, LANES), jnp.float32)
    if direct:
        volume_out, small = pl.pallas_call(
            functools.partial(volume_kernel, shell_vox, vox_dev, levels),
            out_shape=(out_shape, jax.ShapeDtypeStruct(small.shape, jnp.float32)),
            in_specs=[vmem] * 4,
            out_specs=(vmem, vmem),
            scratch_shapes=[
                total,
                pltpu.VMEM((orients, 3 * classes, pix), jnp.bfloat16),
                pltpu.VMEM((orients - 1, 3 * classes, pix), jnp.bfloat16),
                pltpu.VMEM((levels + 1,) + small.shape, jnp.float32),
                pltpu.VMEM((levels,) + small.shape, jnp.float32),
                pltpu.SemaphoreType.DMA((2 * levels * PARTS,)),
                pltpu.SemaphoreType.DMA((2 * levels * PARTS,)),
                pltpu.SemaphoreType.DMA((levels,)),
                pltpu.SemaphoreType.DMA((levels,)),
            ],
            compiler_params=pltpu.CompilerParams(
                vmem_limit_bytes=BIG, collective_id=2, has_side_effects=True
            ),
        )(slice_index, sums, small, prior_precision)
    else:
        small = lax.psum(small, "dom")
        volume_out = pl.pallas_call(
            functools.partial(scatter_kernel, shell_vox, vox_dev),
            grid=(orients,),
            out_shape=out_shape,
            in_specs=[
                pl.BlockSpec((orients, pix), lambda o: (0, 0)),
                pl.BlockSpec((1, 3 * classes, pix), lambda o: (o, 0, 0)),
                pl.BlockSpec((1, vox_dev), lambda o: (0, 0)),
            ],
            out_specs=pl.BlockSpec((2, classes, vox_dev), lambda o: (0, 0, 0)),
            scratch_shapes=[total],
            compiler_params=params,
        )(slice_index, lax.psum(sums, "dom"), prior_precision)
    particles = part_dev * groups
    noise_update = small[:noise_rows].reshape(pix) / (2.0 * particles)
    occupancy = small[noise_rows:, 0] / particles
    new_volume = jnp.transpose(volume_out, (1, 0, 2))[:, :, None, :]
    return (new_volume, noise_update, occupancy)


def solution(mesh):
    in_specs = (
        P("dom", None, "vol"),
        P("dom", "vol"),
        P("dom", None),
        P("dom", None),
        P(None, "vol"),
        P(None, None, "vol", "dom"),
        P("vol"),
        P(),
        P("vol", "dom"),
    )
    out_specs = (P(None, None, "vol", "dom"), P("vol"), P())
    return jax.shard_map(shards, mesh=mesh, in_specs=in_specs, out_specs=out_specs, check_vma=False)
```

```python
import functools

import jax
import jax.numpy as jnp
from jax import lax
from jax.experimental import pallas as pl
from jax.experimental.pallas import tpu as pltpu
from jax.sharding import PartitionSpec as P

LANES = 256
BIG = 48 << 20
NT = (((1,), (1,)), ((), ()))


def voxel_base(shell_vox, vox_dev):
    return lax.axis_index("vol") * shell_vox + lax.axis_index("dom") * vox_dev


def gather_kernel(shell_vox, vox_dev, index_ref, vol_ref, out_ref, stack_ref):
    orient = pl.program_id(0)
    groups = vox_dev // LANES
    rows = vol_ref.shape[0]

    @pl.when(orient == 0)
    def _():
        for q in range(groups):
            stack_ref[q * rows : (q + 1) * rows, :] = vol_ref[:, q * LANES : (q + 1) * LANES]

    rel = index_ref[pl.ds(orient, 1), :] - voxel_base(shell_vox, vox_dev)
    low = rel & (LANES - 1)
    high = rel >> 8
    pix = rel.shape[1]
    step = 256
    for start in range(0, pix, step):
        low_c = low[:, start : start + step]
        high_c = high[:, start : start + step]
        hot = jnp.where(
            lax.broadcasted_iota(jnp.int32, (LANES, step), 0) == low_c, 1.0, 0.0
        ).astype(jnp.bfloat16)
        found = jnp.dot(stack_ref[...], hot, preferred_element_type=jnp.float32)
        total = jnp.zeros((rows, step), jnp.float32)
        for q in range(groups):
            total = jnp.where(high_c == q, found[q * rows : (q + 1) * rows], total)
        out_ref[0, :, start : start + step] = total.astype(jnp.bfloat16)


def scatter_kernel(shell_vox, vox_dev, index_ref, table_ref, prior_ref, out_ref, total_ref):
    orient = pl.program_id(0)
    groups = vox_dev // LANES
    rows = table_ref.shape[1]

    @pl.when(orient == 0)
    def _():
        total_ref[...] = jnp.zeros_like(total_ref)

    rel = index_ref[pl.ds(orient, 1), :] - voxel_base(shell_vox, vox_dev)
    low = rel & (LANES - 1)
    high = rel >> 8
    pix = rel.shape[1]
    hot = jnp.where(
        lax.broadcasted_iota(jnp.int32, (LANES, pix), 0) == low, 1.0, 0.0
    ).astype(jnp.bfloat16)
    table = table_ref[0]
    parts = [
        table * jnp.where(high == q, 1.0, 0.0).astype(jnp.bfloat16) for q in range(groups)
    ]
    spread = jnp.concatenate(parts, axis=0) if groups > 1 else parts[0]
    total_ref[...] += lax.dot_general(spread, hot, NT, preferred_element_type=jnp.float32)

    @pl.when(orient == pl.num_programs(0) - 1)
    def _():
        third = rows // 3
        for q in range(groups):
            cols = slice(q * LANES, (q + 1) * LANES)
            at = q * rows
            weight = total_ref[at + 2 * third : at + rows, :] + prior_ref[:, cols]
            out_ref[0, :, cols] = (total_ref[at : at + third, :] / weight).astype(jnp.bfloat16)
            out_ref[1, :, cols] = (total_ref[at + third : at + 2 * third, :] / weight).astype(
                jnp.bfloat16
            )


MESH = pl.DeviceIdType.MESH
PARTS = 2


def level_bit(level):
    me = lax.axis_index("dom")
    return lax.rem(me // (1 << level), 2)


def partner(level):
    return lax.axis_index("dom") + (1 - 2 * level_bit(level)) * (1 << level)


def greet(levels):
    barrier = pltpu.get_barrier_semaphore()
    for level in range(levels):
        pl.semaphore_signal(barrier, inc=1, device_id={"dom": partner(level)}, device_id_type=MESH)
    pl.semaphore_wait(barrier, levels)


def send(src, dst, send_sem, recv_sem, at, level):
    copy = pltpu.make_async_remote_copy(
        src_ref=src,
        dst_ref=dst,
        send_sem=send_sem.at[at],
        recv_sem=recv_sem.at[at],
        device_id={"dom": partner(level)},
        device_id_type=MESH,
    )
    copy.start()
    return copy


class Exchange:
    def __init__(self, levels, first_ref, full_ref, recv_ref, send_sem, recv_sem):
        self.levels = levels
        self.first, self.full, self.recv = first_ref, full_ref, recv_ref
        self.sems = (send_sem, recv_sem)
        self.width = full_ref.shape[2] // PARTS
        self.low = [0]
        self.size = [1 << levels]
        for level in range(levels):
            half = self.size[-1] // 2
            self.low.append(self.low[-1] + level_bit(level) * half)
            self.size.append(half)
        self.slot = [self.size[0] - self.size[level] for level in range(levels)]

    def cols(self, part):
        return pl.ds(part * self.width, self.width)

    def source(self, level, at):
        if level == 0:
            return self.first, at
        return self.recv, self.slot[level - 1] + at - self.low[level]

    def scatter_start(self, level, part):
        half = self.size[level + 1]
        source, away = self.source(level, self.fresh(level))
        return send(
            source.at[pl.ds(away, half), :, self.cols(part)],
            self.recv.at[pl.ds(self.slot[level], half), :, self.cols(part)],
            *self.sems,
            level * PARTS + part,
            level,
        )

    def scatter_add(self, level, part):
        half = self.size[level + 1]
        for i in range(half):
            source, at = self.source(level, self.low[level + 1] + i)
            slot = self.slot[level] + i
            total = source[at, :, self.cols(part)] + self.recv[slot, :, self.cols(part)]
            if half > 1:
                self.recv[slot, :, self.cols(part)] = total
            else:
                self.full[self.low[level + 1], :, self.cols(part)] = total

    def gather_start(self, level, part):
        held = pl.ds(self.low[level + 1], self.size[level + 1])
        view = self.full.at[held, :, self.cols(part)]
        return send(
            view, view, *self.sems, (self.levels + level) * PARTS + part, level
        )

    def fresh(self, level):
        return self.low[level] + (1 - level_bit(level)) * self.size[level + 1]


def exchange_table(
    shell_vox, vox_dev, levels, index_ref, vol_ref, full_ref,
    stack_ref, first_ref, recv_ref, send_sem, recv_sem, prepare, chunks,
):
    groups = vox_dev // LANES
    rows = vol_ref.shape[0]
    pix = index_ref.shape[1]
    step = 256
    for q in range(groups):
        stack_ref[q * rows : (q + 1) * rows, :] = vol_ref[:, q * LANES : (q + 1) * LANES]
    base = voxel_base(shell_vox, vox_dev)

    def lookup(orient):
        rel = index_ref[pl.ds(orient, 1), :] - base
        low = rel & (LANES - 1)
        high = rel >> 8
        for start in range(0, pix, step):
            low_c = low[:, start : start + step]
            high_c = high[:, start : start + step]
            hot = jnp.where(
                lax.broadcasted_iota(jnp.int32, (LANES, step), 0) == low_c, 1.0, 0.0
            ).astype(jnp.bfloat16)
            found = jnp.dot(stack_ref[...], hot, preferred_element_type=jnp.float32)
            total = jnp.zeros((rows, step), jnp.float32)
            for q in range(groups):
                total = jnp.where(high_c == q, found[q * rows : (q + 1) * rows], total)
            first_ref[orient, :, start : start + step] = total.astype(jnp.bfloat16)

    ex = Exchange(levels, first_ref, full_ref, recv_ref, send_sem, recv_sem)
    half = ex.size[1]
    away = ex.fresh(0)

    @pl.loop(0, half)
    def _(i):
        lookup(away + i)

    copies = [ex.scatter_start(0, part) for part in range(PARTS)]

    @pl.loop(0, half)
    def _(i):
        lookup(ex.low[1] + i)

    for level in range(levels):
        if level == 1:
            pl.loop(0, chunks // 2)(prepare)
        for part in range(PARTS):
            copies[part].wait()
            ex.scatter_add(level, part)
            if level + 1 < levels:
                copies[part] = ex.scatter_start(level + 1, part)
            else:
                copies[part] = ex.gather_start(level, part)
    for level in range(levels - 1, -1, -1):
        if level == min(1, levels - 1):
            pl.loop(chunks // 2, chunks)(prepare)
        for part in range(PARTS):
            copies[part].wait()
            if level > 0:
                copies[part] = ex.gather_start(level - 1, part)


def volume_kernel(
    shell_vox, vox_dev, levels, index_ref, first_ref, small_ref, prior_ref,
    out_ref, small_out_ref,
    total_ref, full_ref, recv_ref, held_ref, got_ref, send_sem, recv_sem, small_send, small_recv,
):
    groups = vox_dev // LANES
    rows = first_ref.shape[1]
    pix = index_ref.shape[1]
    greet(levels)
    base = voxel_base(shell_vox, vox_dev)
    ex = Exchange(levels, first_ref, full_ref, recv_ref, send_sem, recv_sem)
    copies = [ex.scatter_start(0, part) for part in range(PARTS)]
    held_ref[0] = small_ref[...]
    small = send(held_ref.at[0], got_ref.at[0], small_send, small_recv, 0, 0)
    total_ref[...] = jnp.zeros_like(total_ref)

    def spread(orient):
        rel = index_ref[pl.ds(orient, 1), :] - base
        low = rel & (LANES - 1)
        high = rel >> 8
        hot = jnp.where(
            lax.broadcasted_iota(jnp.int32, (LANES, pix), 0) == low, 1.0, 0.0
        ).astype(jnp.bfloat16)
        table = full_ref[orient]
        parts = [
            table * jnp.where(high == q, 1.0, 0.0).astype(jnp.bfloat16) for q in range(groups)
        ]
        wide = jnp.concatenate(parts, axis=0) if groups > 1 else parts[0]
        total_ref[...] += lax.dot_general(wide, hot, NT, preferred_element_type=jnp.float32)

    for level in range(levels):
        for part in range(PARTS):
            copies[part].wait()
            ex.scatter_add(level, part)
            if level + 1 < levels:
                copies[part] = ex.scatter_start(level + 1, part)
            else:
                copies[part] = ex.gather_start(level, part)
        small.wait()
        held_ref[level + 1] = held_ref[level] + got_ref[level]
        if level + 1 < levels:
            small = send(
                held_ref.at[level + 1], got_ref.at[level + 1], small_send, small_recv,
                level + 1, level + 1,
            )
    small_out_ref[...] = held_ref[levels]
    spread(ex.low[levels])
    for level in range(levels - 1, -1, -1):
        for part in range(PARTS):
            copies[part].wait()
            if level > 0:
                copies[part] = ex.gather_start(level - 1, part)

        @pl.loop(0, ex.size[level + 1])
        def _(i, level=level):
            spread(ex.fresh(level) + i)

    third = rows // 3
    for q in range(groups):
        cols = slice(q * LANES, (q + 1) * LANES)
        at = q * rows
        weight = total_ref[at + 2 * third : at + rows, :] + prior_ref[:, cols]
        out_ref[0, :, cols] = (total_ref[at : at + third, :] / weight).astype(jnp.bfloat16)
        out_ref[1, :, cols] = (total_ref[at + third : at + 2 * third, :] / weight).astype(
            jnp.bfloat16
        )


def particle_kernel(
    peers, dims, prior_ref, hypo_ref, image0_ref, image1_ref, gain_ref, noise_ref, index_ref,
    source_ref, out_ref, small_ref, fits_ref, weighted_ref, damped_ref, carried_ref, square_ref,
    energy_ref, send_sem, recv_sem, *scratch,
):
    me = lax.axis_index("vol")
    barrier = pltpu.get_barrier_semaphore()
    greeted = peers - 1
    if dims is not None:
        greeted += dims[2]
        for level in range(dims[2]):
            pl.semaphore_signal(
                barrier, inc=1, device_id={"dom": partner(level)}, device_id_type=MESH
            )
    for hop in range(1, peers):
        other = lax.rem(me + hop, peers)
        pl.semaphore_signal(barrier, inc=1, device_id={"vol": other}, device_id_type=MESH)
    pl.semaphore_wait(barrier, greeted)
    inverse = 1.0 / noise_ref[...]
    energy_ref[...] = jnp.zeros_like(energy_ref)
    block = 32
    chunks = gain_ref.shape[0] // block

    def prepare(i):
        rows = pl.ds(pl.multiple_of(i * block, block), block)
        gain = gain_ref[rows, :].astype(jnp.float32)
        square = gain * gain
        square_ref[rows, :] = square.astype(jnp.bfloat16)
        damped_ref[rows, :] = (square * (0.5 * inverse)).astype(jnp.bfloat16)
        power = jnp.zeros(gain.shape, jnp.float32)
        for r, image_ref in enumerate((image0_ref, image1_ref)):
            image = image_ref[rows, :].astype(jnp.float32)
            power += image * image
            product = gain * image
            carried_ref[r, rows, :] = product.astype(jnp.bfloat16)
            weighted_ref[r, rows, :] = (product * inverse).astype(jnp.bfloat16)
        energy_ref[...] += jnp.sum(power.reshape(block // 8, 8, -1), axis=0)

    if dims is None:
        table_ref = source_ref
        pl.loop(0, chunks)(prepare)
    else:
        table_ref = scratch[0]
        exchange_table(*dims, index_ref, source_ref, *scratch, prepare, chunks)
    orients, double, pix = table_ref.shape
    classes = double // 2
    count = orients * classes
    step = 256
    hypo = hypo_ref[...]
    value = jnp.zeros((count, hypo.shape[1]), jnp.float32)

    def views(cols):
        p0 = table_ref[:, :classes, cols].reshape(count, step)
        p1 = table_ref[:, classes:, cols].reshape(count, step)
        f0 = p0.astype(jnp.float32)
        f1 = p1.astype(jnp.float32)
        return p0, p1, f0, f1, (f0 * f0 + f1 * f1).astype(jnp.bfloat16)

    for start in range(0, pix, step):
        cols = slice(start, start + step)
        p0, p1, _, _, power = views(cols)
        value += lax.dot_general(p0, weighted_ref[0, :, cols], NT, preferred_element_type=jnp.float32)
        value += lax.dot_general(p1, weighted_ref[1, :, cols], NT, preferred_element_type=jnp.float32)
        value -= lax.dot_general(power, damped_ref[:, cols], NT, preferred_element_type=jnp.float32)
    ids = lax.broadcasted_iota(jnp.int32, value.shape, 0)
    rows = [
        jnp.sum(jnp.where(hypo[k : k + 1, :] == ids, value, 0.0), axis=0, keepdims=True)
        for k in range(hypo.shape[0])
    ]
    fits_ref[me] = jnp.concatenate(rows, axis=0)
    copies = []
    for hop in range(1, peers):
        copy = pltpu.make_async_remote_copy(
            src_ref=fits_ref.at[me],
            dst_ref=fits_ref.at[me],
            send_sem=send_sem.at[hop - 1],
            recv_sem=recv_sem.at[hop - 1],
            device_id={"vol": lax.rem(me + hop, peers)},
            device_id_type=MESH,
        )
        copy.start()
        copies.append(copy)
    class_of = lax.rem(hypo, classes)
    scores = jnp.zeros(hypo.shape, jnp.float32)
    for c in range(classes):
        scores += jnp.where(class_of == c, prior_ref[c], 0.0)
    for copy in copies:
        copy.wait()
    fit = fits_ref[0]
    for peer in range(1, peers):
        fit += fits_ref[peer]
    scores += fit
    top = jnp.max(scores, axis=0, keepdims=True)
    expo = jnp.exp(scores - top)
    posterior = expo / jnp.sum(expo, axis=0, keepdims=True)
    member = jnp.zeros(ids.shape, jnp.float32)
    for k in range(hypo.shape[0]):
        member += jnp.where(hypo[k : k + 1, :] == ids, posterior[k : k + 1, :], 0.0)
    occ = jnp.sum(member, axis=1, keepdims=True)
    occ = jnp.sum(occ.reshape(orients, classes, 1), axis=0)
    noise_rows = pix // 128
    small_ref[noise_rows:, :] = jnp.broadcast_to(occ, (classes, 128))
    member16 = member.astype(jnp.bfloat16)
    for start in range(0, pix, step):
        cols = slice(start, start + step)
        _, _, f0, f1, power = views(cols)
        d0 = jnp.dot(member16, carried_ref[0, :, cols], preferred_element_type=jnp.float32)
        d1 = jnp.dot(member16, carried_ref[1, :, cols], preferred_element_type=jnp.float32)
        dw = jnp.dot(member16, square_ref[:, cols], preferred_element_type=jnp.float32)
        noise = jnp.sum(energy_ref[:, cols], axis=0, keepdims=True) + jnp.sum(
            power.astype(jnp.float32) * dw - 2.0 * (f0 * d0 + f1 * d1), axis=0, keepdims=True
        )
        for i in range(step // 128):
            row = start // 128 + i
            small_ref[row : row + 1, :] = noise[:, i * 128 : (i + 1) * 128]
        for i, d in enumerate((d0, d1, dw)):
            out_ref[:, i * classes : (i + 1) * classes, cols] = d.astype(jnp.bfloat16).reshape(
                orients, classes, step
            )


def shards(
    images,
    ctf_gain,
    orientation,
    class_ids,
    slice_index,
    volume,
    noise_power,
    log_prior,
    prior_precision,
):
    groups = lax.axis_size("dom")
    peers = lax.axis_size("vol")
    part_dev = images.shape[0]
    pix = images.shape[2]
    classes = volume.shape[0]
    vox_dev = volume.shape[3]
    orients = slice_index.shape[0]
    shell_vox = vox_dev * groups
    cands = orientation.shape[1]
    levels = groups.bit_length() - 1
    direct = groups == orients and groups == 1 << levels
    params = pltpu.CompilerParams(vmem_limit_bytes=BIG)
    vmem = pl.BlockSpec(memory_space=pltpu.VMEM)
    vol_rows = jnp.transpose(volume[:, :, 0, :], (1, 0, 2)).reshape(2 * classes, vox_dev)
    stack = pltpu.VMEM((2 * classes * vox_dev // LANES, LANES), jnp.bfloat16)
    particle_scratch = [
        pltpu.VMEM((peers, cands, part_dev), jnp.float32),
        pltpu.VMEM((2, part_dev, pix), jnp.bfloat16),
        pltpu.VMEM((part_dev, pix), jnp.bfloat16),
        pltpu.VMEM((2, part_dev, pix), jnp.bfloat16),
        pltpu.VMEM((part_dev, pix), jnp.bfloat16),
        pltpu.VMEM((8, pix), jnp.float32),
        pltpu.SemaphoreType.DMA((peers - 1,)),
        pltpu.SemaphoreType.DMA((peers - 1,)),
    ]
    dims = None
    source = vol_rows
    if direct:
        dims = (shell_vox, vox_dev, levels)
        particle_scratch += [
            pltpu.VMEM((orients, 2 * classes, pix), jnp.bfloat16),
            stack,
            pltpu.VMEM((orients, 2 * classes, pix), jnp.bfloat16),
            pltpu.VMEM((orients - 1, 2 * classes, pix), jnp.bfloat16),
            pltpu.SemaphoreType.DMA((2 * levels * PARTS,)),
            pltpu.SemaphoreType.DMA((2 * levels * PARTS,)),
        ]
    else:
        found = pl.pallas_call(
            functools.partial(gather_kernel, shell_vox, vox_dev),
            grid=(orients,),
            out_shape=jax.ShapeDtypeStruct((orients, 2 * classes, pix), jnp.bfloat16),
            in_specs=[
                pl.BlockSpec((orients, pix), lambda o: (0, 0)),
                pl.BlockSpec((2 * classes, vox_dev), lambda o: (0, 0)),
            ],
            out_specs=pl.BlockSpec((1, 2 * classes, pix), lambda o: (o, 0, 0)),
            scratch_shapes=[stack],
            compiler_params=params,
        )(slice_index, vol_rows)
        source = lax.psum(found, "dom")

    hypo = (orientation * classes + class_ids).T
    noise_rows = pix // 128
    sums, small = pl.pallas_call(
        functools.partial(particle_kernel, peers, dims),
        out_shape=(
            jax.ShapeDtypeStruct((orients, 3 * classes, pix), jnp.bfloat16),
            jax.ShapeDtypeStruct((noise_rows + classes, 128), jnp.float32),
        ),
        in_specs=[pl.BlockSpec(memory_space=pltpu.SMEM)] + [vmem] * 7,
        out_specs=(vmem, vmem),
        scratch_shapes=particle_scratch,
        compiler_params=pltpu.CompilerParams(
            vmem_limit_bytes=BIG, collective_id=1, has_side_effects=True
        ),
    )(
        log_prior, hypo, images[:, 0, :], images[:, 1, :], ctf_gain, noise_power[None, :],
        slice_index, source,
    )
    out_shape = jax.ShapeDtypeStruct((2, classes, vox_dev), jnp.bfloat16)
    total = pltpu.VMEM((3 * classes * vox_dev // LANES, LANES), jnp.float32)
    if direct:
        volume_out, small = pl.pallas_call(
            functools.partial(volume_kernel, shell_vox, vox_dev, levels),
            out_shape=(out_shape, jax.ShapeDtypeStruct(small.shape, jnp.float32)),
            in_specs=[vmem] * 4,
            out_specs=(vmem, vmem),
            scratch_shapes=[
                total,
                pltpu.VMEM((orients, 3 * classes, pix), jnp.bfloat16),
                pltpu.VMEM((orients - 1, 3 * classes, pix), jnp.bfloat16),
                pltpu.VMEM((levels + 1,) + small.shape, jnp.float32),
                pltpu.VMEM((levels,) + small.shape, jnp.float32),
                pltpu.SemaphoreType.DMA((2 * levels * PARTS,)),
                pltpu.SemaphoreType.DMA((2 * levels * PARTS,)),
                pltpu.SemaphoreType.DMA((levels,)),
                pltpu.SemaphoreType.DMA((levels,)),
            ],
            compiler_params=pltpu.CompilerParams(
                vmem_limit_bytes=BIG, collective_id=2, has_side_effects=True
            ),
        )(slice_index, sums, small, prior_precision)
    else:
        small = lax.psum(small, "dom")
        volume_out = pl.pallas_call(
            functools.partial(scatter_kernel, shell_vox, vox_dev),
            grid=(orients,),
            out_shape=out_shape,
            in_specs=[
                pl.BlockSpec((orients, pix), lambda o: (0, 0)),
                pl.BlockSpec((1, 3 * classes, pix), lambda o: (o, 0, 0)),
                pl.BlockSpec((1, vox_dev), lambda o: (0, 0)),
            ],
            out_specs=pl.BlockSpec((2, classes, vox_dev), lambda o: (0, 0, 0)),
            scratch_shapes=[total],
            compiler_params=params,
        )(slice_index, lax.psum(sums, "dom"), prior_precision)
    particles = part_dev * groups
    noise_update = small[:noise_rows].reshape(pix) / (2.0 * particles)
    occupancy = small[noise_rows:, 0] / particles
    new_volume = jnp.transpose(volume_out, (1, 0, 2))[:, :, None, :]
    return (new_volume, noise_update, occupancy)


def solution(mesh):
    in_specs = (
        P("dom", None, "vol"),
        P("dom", "vol"),
        P("dom", None),
        P("dom", None),
        P(None, "vol"),
        P(None, None, "vol", "dom"),
        P("vol"),
        P(),
        P("vol", "dom"),
    )
    out_specs = (P(None, None, "vol", "dom"), P("vol"), P())
    return jax.shard_map(shards, mesh=mesh, in_specs=in_specs, out_specs=out_specs, check_vma=False)
```
